256 devices in a mesh: seq: 32 (over z, x), kvh: 8 (over y, core).
Axes of the slice: x: 4, y: 4, z: 8, core: 2. Of those that a mesh axis runs over, the one named last changes fastest.
Arguments:
- queries: bfloat16 [32768, 4096], P('seq', 'kvh'), may hold values from -12 to 12
- kv_cache: bfloat16 [2, 262144, 1024], P(None, 'seq', 'kvh'), may hold values from -6 to 6
- selected: int32 [256, 8, 2], P('seq', 'kvh'), may hold values from 0 to 254, as said below
- out_weight: bfloat16 [4096, 4096], P('kvh', 'seq'), may hold values from -0.125 to 0.125
Outputs:
- output: bfloat16 [32768, 4096], P('seq', 'kvh')
The draws below stay inside these ranges and needn't reach their ends.
Inputs may be any that keep to these rules, and one draw needn't show every extreme that they name: `selected`: for each KV head, the 16 blocks named by the tiles of one device of seq lie in the ranges of distinct devices (block b lies in the range of device b // 8); for each KV head, some device's range is named by a tile of every device.
All inputs are finite; a program needn't handle non-finite values.
Results may differ from the reference program's by a relative error of at most 0.017.
Values may be sent and summed in bfloat16 or wider, within the bound.
A program may use at most 128 MiB of HBM per device.

```python
import jax
import jax.numpy as jnp
from jax import lax

GROUP = 4
HD = 128
DOUT = 4096
BLK = 1024
TILE = 128
SEL = 2
KVB_DEV = 8
QT_DEV = 1024
KVH = 8
H = 32
TPD = 8
TILES = 256
QTOK = 32768
NB = 256


def draw_queries(key, part):
    noise_key = jax.random.fold_in(key, 11)
    return (jnp.clip(jax.random.normal(noise_key, (QTOK, H * HD), jnp.float32), -6.0, 6.0) * 2.0).astype(jnp.bfloat16)


def draw_kv_cache(key, part):
    noise_key = jax.random.fold_in(key, 13)
    return jnp.clip(jax.random.normal(noise_key, (2, NB * BLK, KVH * HD), jnp.float32), -6.0, 6.0).astype(jnp.bfloat16)


def draw_selected(key, part):
    devices = NB // KVB_DEV
    wanted = TPD * SEL
    base_key = jax.random.fold_in(key, 17)
    key_hot, key_favour, key_noise, key_order, key_first, key_second = jax.random.split(base_key, 6)
    hottest = jax.random.randint(key_hot, (KVH,), 0, devices)
    favour = jax.random.randint(key_favour, (devices,), 0, 4)
    noise = jax.random.randint(key_noise, (devices, KVH, devices), 0, 4096)
    owner_ids = jnp.arange(devices)
    boost = (owner_ids[None, None, :] == hottest[None, :, None]).astype(jnp.int32) * (1 << 20)
    score = (noise + favour[None, None, :] * 2048 + boost) * devices + owner_ids[None, None, :]
    unused, chosen = lax.top_k(score, wanted)
    shuffle = jax.random.randint(key_order, (devices, KVH, wanted), 0, 4096) * wanted + jnp.arange(wanted)
    order = jnp.argsort(shuffle, axis=-1)
    owners = jnp.take_along_axis(chosen, order, axis=-1).astype(jnp.int32)
    source = jnp.arange(devices, dtype=jnp.int32)[:, None, None]
    count = jnp.where(owners == source, KVB_DEV - 1, KVB_DEV)
    first_pick = jax.random.randint(key_first, (devices, KVH, wanted), 0, 1 << 16) % count
    second_pick = jax.random.randint(key_second, (devices, KVH, wanted), 0, 1 << 16) % count
    within = jnp.minimum(first_pick, second_pick)
    block = owners * KVB_DEV + within
    own_block = source * KVB_DEV + KVB_DEV - 1
    entry = jnp.where(block > own_block, block - 1, block)
    entry = entry.reshape(devices, KVH, TPD, SEL).transpose(0, 2, 1, 3).reshape(TILES, KVH, SEL)
    return entry.astype(jnp.int32)


def block_levels(stream_key, dims, cuts, least, high):
    level = 1.0
    for dim, shards_of in cuts:
        heights = jax.random.uniform(jax.random.fold_in(jax.random.fold_in(stream_key, 6), dim), (shards_of,), jnp.float32, least / len(cuts), high / len(cuts))
        level = level * jnp.repeat(jnp.exp(heights), dims[dim] // shards_of).reshape((-1,) + (1,) * (len(dims) - 1 - dim))
    return level


def normal_values(key, shape, scale, reach, cuts=(), kind=jnp.bfloat16):
    result = scale * jax.random.normal(key, shape, jnp.float32)
    if cuts:
        result = result * block_levels(key, shape, cuts, -0.22, 0.18)
    return jnp.clip(result, -reach, reach).astype(kind)


def setup_inputs(seed: int = 0) -> dict:
    splits = jax.random.split(jax.random.key(seed), 5)
    return {
        "queries": draw_queries(jax.random.fold_in(splits[4], 71), 0),
        "kv_cache": draw_kv_cache(jax.random.fold_in(splits[4], 71), 0),
        "selected": draw_selected(jax.random.fold_in(splits[4], 71), 0),
        "out_weight": normal_values(splits[3], (H * HD, DOUT), (H * HD // 2) ** -0.5, 0.125, ((0, 8), (1, 32))),
    }


def attend(query_tile, key_rows, value_rows, visible):
    scores = jnp.einsum("igd,kd->gik", query_tile.astype(jnp.float32), key_rows.astype(jnp.float32)) * (HD ** -0.5)
    scores = jnp.where(visible[None], scores, -jnp.inf)
    row_max = jnp.max(scores, axis=2)
    weights = jnp.exp(scores - row_max[:, :, None])
    row_sum = jnp.sum(weights, axis=2)
    rounded = lax.optimization_barrier(weights.astype(jnp.bfloat16)).astype(jnp.float32)
    summed = jnp.einsum("gik,kd->gid", rounded, value_rows.astype(jnp.float32))
    return row_max, row_sum, (summed / row_sum[:, :, None]).astype(jnp.bfloat16)


def combine(row_maxes, row_sums, normeds):
    highest = row_maxes[0]
    for extra in row_maxes[1:]:
        highest = jnp.maximum(highest, extra)
    norm_sum = jnp.zeros_like(highest)
    blended = jnp.zeros(normeds[0].shape, highest.dtype)
    for top_value, sum_value, normed in zip(row_maxes, row_sums, normeds):
        factor = jnp.exp(top_value - highest) * sum_value
        norm_sum = norm_sum + factor
        blended = blended + factor[..., None] * normed.astype(highest.dtype)
    return blended / norm_sum[..., None]


def reference(queries, kv_cache, selected, out_weight):
    tiles_dev = QT_DEV // TILE
    key_offsets = jnp.arange(BLK)
    full_view = jnp.ones((TILE, BLK), dtype=bool)

    def one_tile(tile):
        device = tile // tiles_dev
        place = tile % tiles_dev
        own_block = device * KVB_DEV + KVB_DEV - 1
        query_rows = lax.dynamic_slice_in_dim(queries, (tile * TILE).astype(jnp.int32), TILE, 0)
        query_offsets = BLK - QT_DEV + place * TILE + jnp.arange(TILE)
        causal = key_offsets[None, :] <= query_offsets[:, None]
        results = []
        for head in range(KVH):
            query_tile = query_rows[:, head * GROUP * HD:(head + 1) * GROUP * HD].reshape(TILE, GROUP, HD)
            chosen = [own_block]
            for pick in range(SEL):
                entry = selected[tile, head, pick]
                chosen.append(jnp.where(entry >= own_block, entry + 1, entry))
            maxima, sums, outs = [], [], []
            for index, block in enumerate(chosen):
                start = (block * BLK).astype(jnp.int32)
                pair = lax.dynamic_slice(kv_cache, (jnp.int32(0), start, jnp.int32(head * HD)), (2, BLK, HD))
                visible = causal if index == 0 else full_view
                top_value, sum_value, normed = attend(query_tile, pair[0], pair[1], visible)
                maxima.append(top_value)
                sums.append(sum_value)
                outs.append(normed)
            mixed = combine(maxima, sums, outs)
            results.append(jnp.transpose(mixed, (1, 0, 2)).reshape(TILE, GROUP * HD))
        return jnp.concatenate(results, axis=1).astype(jnp.bfloat16)

    attention = lax.map(one_tile, jnp.arange(TILES, dtype=jnp.int32)).reshape(QTOK, H * HD)
    total = jnp.zeros((QTOK, DOUT), jnp.float32)
    for head in range(KVH):
        lower = head * GROUP * HD
        upper = (head + 1) * GROUP * HD
        term = jnp.dot(attention[:, lower:upper], out_weight[lower:upper], preferred_element_type=jnp.float32)
        total = total + lax.optimization_barrier(term.astype(jnp.bfloat16)).astype(jnp.float32)
    return total.astype(jnp.bfloat16)
```

```python
import functools

import jax
import jax.numpy as jnp
from jax import lax
from jax.experimental import pallas as pl
from jax.experimental.pallas import tpu as pltpu
from jax.sharding import PartitionSpec as P

GROUP = 4
HD = 128
BLK = 1024
TILE = 128
SEL = 2
ZN = 8
XN = 4
SEQ = ZN * XN
KVN = 8
YN = 4
TILES = 8
BLOCKS = 8
SCALE = HD ** (-0.5)
LOG2E = 1.4426950408889634
MESH = pl.DeviceIdType.MESH
ROUNDS = ((0, 1), (1, 1), (2, 1), (3, 1))


def to_row(column, eye):
    return jnp.sum(jnp.where(eye, column, 0.0), axis=0, keepdims=True)


def to_column(row, eye):
    return jnp.sum(jnp.where(eye, row, 0.0), axis=1, keepdims=True)


def attend(query, keys, values, visible):
    scores = lax.dot_general(
        query, keys, (((1,), (1,)), ((), ())), preferred_element_type=jnp.float32
    )
    if visible is not None:
        scores = jnp.where(visible, scores, -jnp.inf)
    top = jnp.max(scores, axis=1, keepdims=True)
    weights = jnp.exp2((scores - top) * (SCALE * LOG2E))
    total = jnp.sum(weights, axis=1, keepdims=True)
    summed = jnp.dot(
        weights.astype(jnp.bfloat16), values, preferred_element_type=jnp.float32
    )
    return (summed / total).astype(jnp.bfloat16), top * SCALE + jnp.log(total)


def fused(tab, q_ref, kv_ref, blk_ref, w_ref, out_ref, *scratch):
    rounds = len(ROUNDS)
    in_o, in_l, att, own_att = (
        scratch[n * rounds : (n + 1) * rounds] for n in range(4)
    )
    rest = scratch[4 * rounds :]
    out_q, in_q, out_o, out_l, own_o, own_l, in_blk, blk_s, wbuf, wfull, acc = rest[:11]
    q_send, q_recv, b_send, b_recv, o_send, o_recv, l_send, l_recv = rest[11:19]
    a_send, a_recv, s_send, s_recv, z_send, z_recv, x_send, x_recv, local_sem = rest[19:]
    seq = lax.axis_index("seq")
    kvh = lax.axis_index("kvh")
    z, x = seq // XN, seq % XN
    y, core = kvh // 2, kvh % 2

    def ahead(shift):
        return ((z + shift // XN) % ZN) * XN + (x + shift % XN) % XN

    def behind(shift):
        return ((z + ZN - shift // XN) % ZN) * XN + (x + XN - shift % XN) % XN

    def chip(step):
        return ((y + step) % YN) * 2 + core

    sibling = y * 2 + 1 - core

    barrier = pltpu.get_barrier_semaphore()

    def greet_seq(shift, carry):
        pl.semaphore_signal(
            barrier, inc=1, device_id={"seq": ahead(shift)}, device_id_type=MESH
        )
        return carry

    lax.fori_loop(1, SEQ, greet_seq, 0)
    for peer in [chip(1), chip(2), chip(3), sibling]:
        pl.semaphore_signal(barrier, inc=1, device_id={"kvh": peer}, device_id_type=MESH)
    pl.semaphore_wait(barrier, SEQ - 1 + YN)

    def remote(src, dst, send, recv, **device):
        return pltpu.make_async_remote_copy(
            src_ref=src,
            dst_ref=dst,
            send_sem=send,
            recv_sem=recv,
            device_id=device,
            device_id_type=MESH,
        )

    def blk_copy(shift):
        return remote(
            blk_ref.at[shift], in_blk.at[shift], b_send.at[shift], b_recv.at[shift], seq=ahead(shift)
        )

    def q_copy(index, shift):
        first, count = ROUNDS[index]
        heads = pl.ds(first, count)
        return remote(
            out_q.at[shift, heads],
            in_q.at[shift, heads],
            q_send.at[index, shift],
            q_recv.at[index, shift],
            seq=ahead(shift),
        )

    def o_copy(index, shift):
        first, count = ROUNDS[index]
        return remote(
            out_o.at[shift, pl.ds(first, count)],
            in_o[index].at[shift],
            o_send.at[index, shift],
            o_recv.at[index, shift],
            seq=behind(shift),
        )

    def l_copy(index, shift):
        first, count = ROUNDS[index]
        return remote(
            out_l.at[shift, pl.ds(first, count)],
            in_l[index].at[shift],
            l_send.at[index, shift],
            l_recv.at[index, shift],
            seq=behind(shift),
        )

    def lanes(index, head):
        wide = ROUNDS[index][1] * HD
        return pl.ds(pl.multiple_of(head * wide, wide), wide)

    def a_copy(index, step):
        return remote(
            own_att[index],
            att[index].at[:, lanes(index, kvh)],
            a_send.at[index, step],
            a_recv.at[index, step],
            kvh=chip(step),
        )

    def s_copy(index, step):
        part = att[index].at[:, lanes(index, chip(YN - step))]
        return remote(
            own_att[index] if step == 0 else part,
            part,
            s_send.at[index, step],
            s_recv.at[index, step],
            kvh=sibling,
        )

    def z_copy(way, step):
        block = (z + ZN - step + 1) % ZN if way == 0 else (z + step - 1) % ZN
        part = wbuf.at[x, block]
        return remote(
            part,
            part,
            z_send.at[way, step],
            z_recv.at[way, step],
            seq=((z + 1) % ZN if way == 0 else (z + ZN - 1) % ZN) * XN + x,
        )

    def x_copy(step):
        part = wbuf.at[x]
        return remote(
            part, part, x_send.at[step], x_recv.at[step], seq=z * XN + (x + step) % XN
        )

    z_steps = (ZN // 2, ZN // 2 - 1)

    def z_start(step):
        for way in range(2):
            if step <= z_steps[way]:
                z_copy(way, step).start()

    def z_wait(step):
        for way in range(2):
            if step <= z_steps[way]:
                z_copy(way, step).wait_recv()

    eye = lax.broadcasted_iota(jnp.int32, (TILE, TILE), 0) == lax.broadcasted_iota(
        jnp.int32, (TILE, TILE), 1
    )

    def own_piece(tile, carry):
        visible = lax.broadcasted_iota(jnp.int32, (TILE, BLK), 1) <= (
            tile * TILE + lax.broadcasted_iota(jnp.int32, (TILE, BLK), 0)
        )
        for head in range(GROUP):
            out, lse = attend(
                q_ref[tile, :, head * HD : (head + 1) * HD],
                kv_ref[0, BLOCKS - 1],
                kv_ref[1, BLOCKS - 1],
                visible,
            )
            own_o[tile, head] = out
            own_l[tile, head] = to_row(lse, eye)
        return carry

    def send_blk(shift, carry):
        blk_copy(shift).start()
        return carry

    def send_queries(index):
        first, count = ROUNDS[index]

        def pack(shift, carry):
            tile = tab[shift]
            for head in range(first, first + count):
                out_q[shift, head] = q_ref[tile, :, head * HD : (head + 1) * HD]
            q_copy(index, shift).start()
            return carry

        for head in range(first, first + count):
            in_q[0, head] = q_ref[tab[0], :, head * HD : (head + 1) * HD]
        lax.fori_loop(1, SEQ, pack, 0)

    def serve_round(index):
        first, count = ROUNDS[index]

        def serve(shift, home):
            block = blk_s[shift, 0, 0]
            for head in range(first, first + count):
                out, lse = attend(
                    in_q[shift, head], kv_ref[0, block], kv_ref[1, block], None
                )
                if home:
                    in_o[index][shift, head - first] = out
                    in_l[index][shift, head - first] = to_row(lse, eye)
                else:
                    out_o[shift, head] = out
                    out_l[shift, head] = to_row(lse, eye)

        def step(shift, carry):
            q_copy(index, shift).wait_recv()
            serve(shift, False)
            o_copy(index, shift).start()
            l_copy(index, shift).start()
            return carry

        serve(0, True)
        lax.fori_loop(1, SEQ, step, 0)

    def mix_round(index):
        first, count = ROUNDS[index]

        def arrived(shift, carry):
            o_copy(index, shift).wait_recv()
            l_copy(index, shift).wait_recv()
            return carry

        lax.fori_loop(1, SEQ, arrived, 0)

        def mix(tile, carry):
            one = tab[SEQ + tile * SEL]
            two = tab[SEQ + tile * SEL + 1]
            row = pl.multiple_of(tile * TILE, TILE)
            for head in range(first, first + count):
                at = head - first
                rows = [own_l[tile, head], in_l[index][one, at], in_l[index][two, at]]
                outs = [own_o[tile, head], in_o[index][one, at], in_o[index][two, at]]
                high = jnp.maximum(jnp.maximum(rows[0], rows[1]), rows[2])
                parts = [jnp.exp(r - high) for r in rows]
                norm = parts[0] + parts[1] + parts[2]
                blended = jnp.zeros((TILE, HD), jnp.float32)
                for part, out in zip(parts, outs):
                    blended = blended + to_column(part / norm, eye) * out.astype(jnp.float32)
                own_att[index][pl.ds(row, TILE), at * HD : (at + 1) * HD] = blended.astype(
                    jnp.bfloat16
                )
            return carry

        lax.fori_loop(0, TILES, mix, 0)
        for step in range(1, YN):
            a_copy(index, step).start()
        s_copy(index, 0).start()
        keep(index).start()

    def keep(index):
        return pltpu.make_async_copy(
            own_att[index], att[index].at[:, lanes(index, kvh)], local_sem.at[1 + index]
        )

    def pass_on(index):
        for step in range(1, YN):
            a_copy(index, step).wait_recv()
            s_copy(index, step).start()

    def project(index):
        first, count = ROUNDS[index]
        for step in range(YN):
            s_copy(index, step).wait_recv()
        keep(index).wait()
        last = index == rounds - 1

        def rows_of(tile, carry):
            rows = pl.ds(pl.multiple_of(tile * 256, 256), 256)
            term = jnp.dot(
                att[index][rows, :],
                wfull[first * KVN * HD : (first + count) * KVN * HD, :],
                preferred_element_type=jnp.float32,
            )
            if index > 0:
                term = acc[rows, :] + term
            if last:
                out_ref[rows, :] = term.astype(jnp.bfloat16)
            else:
                acc[rows, :] = term
            return carry

        lax.fori_loop(0, TILES // 2, rows_of, 0)

    wbuf[x, z] = w_ref[...]
    z_start(1)
    lax.fori_loop(1, SEQ, send_blk, 0)
    tiles = TILES // rounds
    for index in range(rounds):
        send_queries(index)
        lax.fori_loop(index * tiles, (index + 1) * tiles, own_piece, 0)
        z_wait(index + 1)
        if index + 1 < rounds:
            z_start(index + 2)
    for step in range(1, XN):
        x_copy(step).start()

    def wait_blk(shift, carry):
        blk_copy(shift).wait_recv()
        return carry

    lax.fori_loop(1, SEQ, wait_blk, 0)
    in_blk[0] = blk_ref[0]
    fetch = pltpu.make_async_copy(in_blk, blk_s, local_sem.at[0])
    fetch.start()
    fetch.wait()

    serve_round(0)
    serve_round(1)
    mix_round(0)
    serve_round(2)
    pass_on(0)
    mix_round(1)
    serve_round(3)
    pass_on(1)
    mix_round(2)

    for step in range(1, XN):
        x_copy(step).wait_recv()
    for index, (first, count) in enumerate(ROUNDS):

        def arrange(head, carry, first=first, count=count):
            row = pl.multiple_of((first * KVN + head * count) * HD, HD)
            for col in range(XN):
                wfull[pl.ds(row, count * HD), col * HD : (col + 1) * HD] = wbuf[
                    col, head, first * HD : (first + count) * HD, :
                ]
            return carry

        lax.fori_loop(0, KVN, arrange, 0)

    project(0)
    project(1)
    pass_on(2)
    mix_round(3)
    project(2)
    pass_on(3)
    project(3)

    for index in range(rounds):

        def finish(shift, carry, index=index):
            q_copy(index, shift).wait_send()
            o_copy(index, shift).wait_send()
            l_copy(index, shift).wait_send()
            return carry

        lax.fori_loop(1, SEQ, finish, 0)
        for step in range(1, YN):
            a_copy(index, step).wait_send()
        for step in range(YN):
            s_copy(index, step).wait_send()

    def finish_blk(shift, carry):
        blk_copy(shift).wait_send()
        return carry

    lax.fori_loop(1, SEQ, finish_blk, 0)
    for way in range(2):
        for step in range(1, z_steps[way] + 1):
            z_copy(way, step).wait_send()
    for step in range(1, XN):
        x_copy(step).wait_send()


def per_device(queries, kv_cache, selected, out_weight):
    rows = queries.shape[0]
    seq = lax.axis_index("seq")
    z, x = seq // XN, seq % XN
    moves = []
    for sz in range(ZN):
        for sx in range(XN):
            for k in range(KVN):
                moves.append(((sz * XN + sx) * KVN + k, (k * XN + sx) * KVN + sz))
    moved = lax.ppermute(out_weight, ("seq", "kvh"), moves)

    own_block = seq * BLOCKS + BLOCKS - 1
    chosen = selected.reshape(TILES * SEL)
    target = jnp.where(chosen >= own_block, chosen + 1, chosen)
    holder = target // BLOCKS
    within = target % BLOCKS
    shift = ((holder // XN - z + ZN) % ZN) * XN + (holder % XN - x + XN) % XN
    routing = shift[None, :] == jnp.arange(SEQ, dtype=jnp.int32)[:, None]
    request_tile = jnp.arange(TILES * SEL, dtype=jnp.int32) // SEL
    slot_tile = jnp.sum(jnp.where(routing, request_tile[None, :], 0), axis=1)
    slot_block = jnp.sum(jnp.where(routing, within[None, :], 0), axis=1)
    table = jnp.concatenate([slot_tile, shift]).astype(jnp.int32)
    slot_block = jnp.broadcast_to(slot_block.astype(jnp.int32)[:, None, None], (SEQ, 1, 128))

    rounds = len(ROUNDS)
    vmem = pl.BlockSpec(memory_space=pltpu.VMEM)
    dma = pltpu.SemaphoreType.DMA
    slots = pltpu.VMEM((SEQ, GROUP, TILE, HD), jnp.bfloat16)
    return pl.pallas_call(
        fused,
        name="fused",
        out_shape=jax.ShapeDtypeStruct((rows, XN * HD), jnp.bfloat16),
        in_specs=[pl.BlockSpec(memory_space=pltpu.SMEM), vmem, vmem, vmem, vmem],
        out_specs=vmem,
        scratch_shapes=[pltpu.VMEM((SEQ, n, TILE, HD), jnp.bfloat16) for _, n in ROUNDS]
        + [pltpu.VMEM((SEQ, n, 1, TILE), jnp.float32) for _, n in ROUNDS]
        + [pltpu.VMEM((rows, KVN * n * HD), jnp.bfloat16) for _, n in ROUNDS]
        + [pltpu.VMEM((rows, n * HD), jnp.bfloat16) for _, n in ROUNDS]
        + [
            slots,
            slots,
            slots,
            pltpu.VMEM((SEQ, GROUP, 1, TILE), jnp.float32),
            pltpu.VMEM((TILES, GROUP, TILE, HD), jnp.bfloat16),
            pltpu.VMEM((TILES, GROUP, 1, TILE), jnp.float32),
            pltpu.VMEM((SEQ, 1, 128), jnp.int32),
            pltpu.SMEM((SEQ, 1, 128), jnp.int32),
            pltpu.VMEM((XN, KVN, GROUP * HD, HD), jnp.bfloat16),
            pltpu.VMEM((KVN * GROUP * HD, XN * HD), jnp.bfloat16),
            pltpu.VMEM((rows, XN * HD), jnp.float32),
        ]
        + [dma((rounds, SEQ))] * 2
        + [dma((SEQ,))] * 2
        + [dma((rounds, SEQ))] * 4
        + [dma((rounds, YN))] * 4
        + [dma((2, ZN))] * 2
        + [dma((XN,))] * 2
        + [dma((1 + rounds,))],
        compiler_params=pltpu.CompilerParams(
            collective_id=0, has_side_effects=True, vmem_limit_bytes=60 << 20
        ),
    )(
        table,
        queries.reshape(TILES, TILE, GROUP * HD),
        kv_cache.reshape(2, BLOCKS, BLK, HD),
        slot_block,
        moved,
    )


def solution(mesh):
    in_specs = (P("seq", "kvh"), P(None, "seq", "kvh"), P("seq", "kvh", None), P("kvh", "seq"))
    out_specs = P("seq", "kvh")
    return jax.shard_map(
        per_device, mesh=mesh, in_specs=in_specs, out_specs=out_specs, check_vma=False
    )
```

```python
import functools

import jax
import jax.numpy as jnp
from jax import lax
from jax.experimental import pallas as pl
from jax.experimental.pallas import tpu as pltpu
from jax.sharding import PartitionSpec as P

GROUP = 4
HD = 128
BLK = 1024
TILE = 128
SEL = 2
ZN = 8
XN = 4
SEQ = ZN * XN
KVN = 8
YN = 4
TILES = 8
BLOCKS = 8
SCALE = HD ** (-0.5)
LOG2E = 1.4426950408889634
MESH = pl.DeviceIdType.MESH
ROUNDS = ((0, 1), (1, 1), (2, 1), (3, 1))


def to_row(column, eye):
    return jnp.sum(jnp.where(eye, column, 0.0), axis=0, keepdims=True)


def to_column(row, eye):
    return jnp.sum(jnp.where(eye, row, 0.0), axis=1, keepdims=True)


def attend(query, keys, values, visible):
    scores = lax.dot_general(
        query, keys, (((1,), (1,)), ((), ())), preferred_element_type=jnp.float32
    )
    if visible is not None:
        scores = jnp.where(visible, scores, -jnp.inf)
    top = jnp.max(scores, axis=1, keepdims=True)
    weights = jnp.exp2((scores - top) * (SCALE * LOG2E))
    total = jnp.sum(weights, axis=1, keepdims=True)
    summed = jnp.dot(
        weights.astype(jnp.bfloat16), values, preferred_element_type=jnp.float32
    )
    return (summed / total).astype(jnp.bfloat16), top * SCALE + jnp.log(total)


def fused(tab, q_ref, cache_ref, blk_ref, w_ref, out_ref, *scratch):
    rounds = len(ROUNDS)
    in_o, in_l, att, own_att = (
        scratch[n * rounds : (n + 1) * rounds] for n in range(4)
    )
    rest = scratch[4 * rounds :]
    out_q, in_q, out_o, out_l, own_o, own_l, in_blk, blk_s, wbuf, wfull, acc, kv_ref = rest[:12]
    q_send, q_recv, b_send, b_recv, o_send, o_recv, l_send, l_recv = rest[12:20]
    a_send, a_recv, s_send, s_recv, z_send, z_recv, x_send, x_recv, p_sem, local_sem = rest[20:]
    seq = lax.axis_index("seq")
    kvh = lax.axis_index("kvh")
    z, x = seq // XN, seq % XN
    y, core = kvh // 2, kvh % 2

    def ahead(shift):
        return ((z + shift // XN) % ZN) * XN + (x + shift % XN) % XN

    def behind(shift):
        return ((z + ZN - shift // XN) % ZN) * XN + (x + XN - shift % XN) % XN

    def chip(step):
        return ((y + step) % YN) * 2 + core

    sibling = y * 2 + 1 - core
    cache = pltpu.make_async_copy(cache_ref, kv_ref, local_sem.at[1 + rounds])
    cache.start()

    barrier = pltpu.get_barrier_semaphore()

    def greet_seq(shift, carry):
        pl.semaphore_signal(
            barrier, inc=1, device_id={"seq": ahead(shift)}, device_id_type=MESH
        )
        return carry

    lax.fori_loop(1, SEQ, greet_seq, 0)
    for peer in [chip(1), chip(2), chip(3), sibling]:
        pl.semaphore_signal(barrier, inc=1, device_id={"kvh": peer}, device_id_type=MESH)
    partner = {"seq": kvh * XN + x, "kvh": z}

    @pl.when(kvh != z)
    def _():
        pl.semaphore_signal(barrier, inc=1, device_id=partner, device_id_type=MESH)
        pl.semaphore_wait(barrier, SEQ + YN)

    @pl.when(kvh == z)
    def _():
        pl.semaphore_wait(barrier, SEQ - 1 + YN)

    def remote(src, dst, send, recv, **device):
        return pltpu.make_async_remote_copy(
            src_ref=src,
            dst_ref=dst,
            send_sem=send,
            recv_sem=recv,
            device_id=device,
            device_id_type=MESH,
        )

    def blk_copy(shift):
        return remote(
            blk_ref.at[shift], in_blk.at[shift], b_send.at[shift], b_recv.at[shift], seq=ahead(shift)
        )

    def q_copy(index, shift):
        first, count = ROUNDS[index]
        heads = pl.ds(first, count)
        return remote(
            out_q.at[shift, heads],
            in_q.at[shift, heads],
            q_send.at[index, shift],
            q_recv.at[index, shift],
            seq=ahead(shift),
        )

    def o_copy(index, shift):
        first, count = ROUNDS[index]
        return remote(
            out_o.at[shift, pl.ds(first, count)],
            in_o[index].at[shift],
            o_send.at[index, shift],
            o_recv.at[index, shift],
            seq=behind(shift),
        )

    def l_copy(index, shift):
        first, count = ROUNDS[index]
        return remote(
            out_l.at[shift, pl.ds(first, count)],
            in_l[index].at[shift],
            l_send.at[index, shift],
            l_recv.at[index, shift],
            seq=behind(shift),
        )

    def lanes(index, head):
        wide = ROUNDS[index][1] * HD
        return pl.ds(pl.multiple_of(head * wide, wide), wide)

    def a_copy(index, step):
        return remote(
            own_att[index],
            att[index].at[:, lanes(index, kvh)],
            a_send.at[index, step],
            a_recv.at[index, step],
            kvh=chip(step),
        )

    def s_copy(index, step):
        part = att[index].at[:, lanes(index, chip(YN - step))]
        return remote(
            own_att[index] if step == 0 else part,
            part,
            s_send.at[index, step],
            s_recv.at[index, step],
            kvh=sibling,
        )

    def z_copy(way, step):
        block = (z + ZN - step + 1) % ZN if way == 0 else (z + step - 1) % ZN
        part = wbuf.at[x, block]
        return remote(
            part,
            part,
            z_send.at[way, step],
            z_recv.at[way, step],
            seq=((z + 1) % ZN if way == 0 else (z + ZN - 1) % ZN) * XN + x,
        )

    def p_copy():
        return remote(w_ref, wbuf.at[x, kvh], p_sem.at[0], p_sem.at[1], **partner)

    def x_copy(piece, step):
        block = (z + ZN - piece) % ZN
        part = wbuf.at[x, block]
        return remote(
            part,
            part,
            x_send.at[piece, step],
            x_recv.at[piece, step],
            seq=z * XN + (x + step) % XN,
        )

    def x_start(*pieces):
        for piece in pieces:
            for step in (2, 1, 3):
                x_copy(piece, step).start()

    z_steps = (ZN // 2, ZN // 2 - 1)

    def z_start(step):
        for way in range(2):
            if step <= z_steps[way]:
                z_copy(way, step).start()

    def z_wait(step):
        for way in range(2):
            if step <= z_steps[way]:
                z_copy(way, step).wait_recv()

    eye = lax.broadcasted_iota(jnp.int32, (TILE, TILE), 0) == lax.broadcasted_iota(
        jnp.int32, (TILE, TILE), 1
    )

    def own_piece(tile, carry):
        visible = lax.broadcasted_iota(jnp.int32, (TILE, BLK), 1) <= (
            tile * TILE + lax.broadcasted_iota(jnp.int32, (TILE, BLK), 0)
        )
        for head in range(GROUP):
            out, lse = attend(
                q_ref[tile, :, head * HD : (head + 1) * HD],
                kv_ref[0, BLOCKS - 1],
                kv_ref[1, BLOCKS - 1],
                visible,
            )
            own_o[tile, head] = out
            own_l[tile, head] = to_row(lse, eye)
        return carry

    def send_blk(shift, carry):
        blk_copy(shift).start()
        return carry

    def send_queries(index):
        first, count = ROUNDS[index]

        def pack(shift, carry):
            tile = tab[shift]
            for head in range(first, first + count):
                out_q[shift, head] = q_ref[tile, :, head * HD : (head + 1) * HD]
            q_copy(index, shift).start()
            return carry

        for head in range(first, first + count):
            in_q[0, head] = q_ref[tab[0], :, head * HD : (head + 1) * HD]
        lax.fori_loop(1, SEQ, pack, 0)

    def serve_round(index, between=()):
        first, count = ROUNDS[index]

        def serve(shift, home):
            block = blk_s[shift, 0, 0]
            for head in range(first, first + count):
                out, lse = attend(
                    in_q[shift, head], kv_ref[0, block], kv_ref[1, block], None
                )
                if home:
                    in_o[index][shift, head - first] = out
                    in_l[index][shift, head - first] = to_row(lse, eye)
                else:
                    out_o[shift, head] = out
                    out_l[shift, head] = to_row(lse, eye)

        def step(shift, carry):
            q_copy(index, shift).wait_recv()
            serve(shift, False)
            o_copy(index, shift).start()
            l_copy(index, shift).start()
            return carry

        serve(0, True)
        cuts = [1 + (SEQ - 1) * n // (len(between) + 1) for n in range(len(between) + 2)]
        for number in range(len(cuts) - 1):
            lax.fori_loop(cuts[number], cuts[number + 1], step, 0)
            if number < len(between):
                piece, distance = between[number]
                x_copy(piece, distance).start()

    def mix_round(index):
        first, count = ROUNDS[index]

        def arrived(shift, carry):
            o_copy(index, shift).wait_recv()
            l_copy(index, shift).wait_recv()
            return carry

        lax.fori_loop(1, SEQ, arrived, 0)

        def mix(tile, carry):
            one = tab[SEQ + tile * SEL]
            two = tab[SEQ + tile * SEL + 1]
            row = pl.multiple_of(tile * TILE, TILE)
            for head in range(first, first + count):
                at = head - first
                rows = [own_l[tile, head], in_l[index][one, at], in_l[index][two, at]]
                outs = [own_o[tile, head], in_o[index][one, at], in_o[index][two, at]]
                high = jnp.maximum(jnp.maximum(rows[0], rows[1]), rows[2])
                parts = [jnp.exp(r - high) for r in rows]
                norm = parts[0] + parts[1] + parts[2]
                blended = jnp.zeros((TILE, HD), jnp.float32)
                for part, out in zip(parts, outs):
                    blended = blended + to_column(part / norm, eye) * out.astype(jnp.float32)
                own_att[index][pl.ds(row, TILE), at * HD : (at + 1) * HD] = blended.astype(
                    jnp.bfloat16
                )
            return carry

        lax.fori_loop(0, TILES, mix, 0)
        for step in range(1, YN):
            a_copy(index, step).start()
        s_copy(index, 0).start()
        keep(index).start()

    def keep(index):
        return pltpu.make_async_copy(
            own_att[index], att[index].at[:, lanes(index, kvh)], local_sem.at[1 + index]
        )

    def pass_on(index):
        for step in range(1, YN):
            a_copy(index, step).wait_recv()
            s_copy(index, step).start()

    def project(index):
        first, count = ROUNDS[index]
        for step in range(YN):
            s_copy(index, step).wait_recv()
        keep(index).wait()
        last = index == rounds - 1

        def rows_of(tile, carry):
            rows = pl.ds(pl.multiple_of(tile * 256, 256), 256)
            term = jnp.dot(
                att[index][rows, :],
                wfull[first * KVN * HD : (first + count) * KVN * HD, :],
                preferred_element_type=jnp.float32,
            )
            if index > 0:
                term = acc[rows, :] + term
            if last:
                out_ref[rows, :] = term.astype(jnp.bfloat16)
            else:
                acc[rows, :] = term
            return carry

        lax.fori_loop(0, TILES // 2, rows_of, 0)

    @pl.when(kvh != z)
    def _():
        p_copy().start()

    @pl.when(kvh == z)
    def _():
        wbuf[x, z] = w_ref[...]

    lax.fori_loop(1, SEQ, send_blk, 0)
    tiles = TILES // rounds
    for index in range(rounds):
        send_queries(index)
        if index == 0:
            cache.wait()
        if index == 1:
            x_start(0)
        if index == 2:
            x_start(1, 7)
        lax.fori_loop(index * tiles, (index + 1) * tiles, own_piece, 0)
        if index == 0:

            @pl.when(kvh != z)
            def _():
                p_copy().wait()

        else:
            z_wait(index)
        z_start(index + 1)

    def wait_blk(shift, carry):
        blk_copy(shift).wait_recv()
        return carry

    lax.fori_loop(1, SEQ, wait_blk, 0)
    in_blk[0] = blk_ref[0]
    fetch = pltpu.make_async_copy(in_blk, blk_s, local_sem.at[0])
    fetch.start()
    fetch.wait()

    serve_round(0, [(p, d) for p in (2, 6) for d in (2, 1, 3)])
    z_wait(rounds)
    serve_round(1, [(p, d) for p in (3, 5) for d in (2, 1, 3)])
    mix_round(0)
    serve_round(2, [(4, d) for d in (2, 1, 3)])
    pass_on(0)
    mix_round(1)
    serve_round(3)
    pass_on(1)
    mix_round(2)

    for piece in range(ZN):
        for step in range(1, XN):
            x_copy(piece, step).wait_recv()
    for index, (first, count) in enumerate(ROUNDS):

        def arrange(head, carry, first=first, count=count):
            row = pl.multiple_of((first * KVN + head * count) * HD, HD)
            for col in range(XN):
                wfull[pl.ds(row, count * HD), col * HD : (col + 1) * HD] = wbuf[
                    col, head, first * HD : (first + count) * HD, :
                ]
            return carry

        lax.fori_loop(0, KVN, arrange, 0)

    project(0)
    project(1)
    pass_on(2)
    mix_round(3)
    project(2)
    pass_on(3)
    project(3)

    for index in range(rounds):

        def finish(shift, carry, index=index):
            q_copy(index, shift).wait_send()
            o_copy(index, shift).wait_send()
            l_copy(index, shift).wait_send()
            return carry

        lax.fori_loop(1, SEQ, finish, 0)
        for step in range(1, YN):
            a_copy(index, step).wait_send()
        for step in range(YN):
            s_copy(index, step).wait_send()

    def finish_blk(shift, carry):
        blk_copy(shift).wait_send()
        return carry

    lax.fori_loop(1, SEQ, finish_blk, 0)
    for way in range(2):
        for step in range(1, z_steps[way] + 1):
            z_copy(way, step).wait_send()
    for piece in range(ZN):
        for step in range(1, XN):
            x_copy(piece, step).wait_send()


def per_device(queries, kv_cache, selected, out_weight):
    rows = queries.shape[0]
    seq = lax.axis_index("seq")
    z, x = seq // XN, seq % XN
    own_block = seq * BLOCKS + BLOCKS - 1
    chosen = selected.reshape(TILES * SEL)
    target = jnp.where(chosen >= own_block, chosen + 1, chosen)
    holder = target // BLOCKS
    within = target % BLOCKS
    shift = ((holder // XN - z + ZN) % ZN) * XN + (holder % XN - x + XN) % XN
    routing = shift[None, :] == jnp.arange(SEQ, dtype=jnp.int32)[:, None]
    request_tile = jnp.arange(TILES * SEL, dtype=jnp.int32) // SEL
    slot_tile = jnp.sum(jnp.where(routing, request_tile[None, :], 0), axis=1)
    slot_block = jnp.sum(jnp.where(routing, within[None, :], 0), axis=1)
    table = jnp.concatenate([slot_tile, shift]).astype(jnp.int32)
    slot_block = jnp.broadcast_to(slot_block.astype(jnp.int32)[:, None, None], (SEQ, 1, 128))

    rounds = len(ROUNDS)
    vmem = pl.BlockSpec(memory_space=pltpu.VMEM)
    dma = pltpu.SemaphoreType.DMA
    slots = pltpu.VMEM((SEQ, GROUP, TILE, HD), jnp.bfloat16)
    return pl.pallas_call(
        fused,
        name="fused",
        out_shape=jax.ShapeDtypeStruct((rows, XN * HD), jnp.bfloat16),
        in_specs=[
            pl.BlockSpec(memory_space=pltpu.SMEM),
            vmem,
            pl.BlockSpec(memory_space=pl.ANY),
            vmem,
            vmem,
        ],
        out_specs=vmem,
        scratch_shapes=[pltpu.VMEM((SEQ, n, TILE, HD), jnp.bfloat16) for _, n in ROUNDS]
        + [pltpu.VMEM((SEQ, n, 1, TILE), jnp.float32) for _, n in ROUNDS]
        + [pltpu.VMEM((rows, KVN * n * HD), jnp.bfloat16) for _, n in ROUNDS]
        + [pltpu.VMEM((rows, n * HD), jnp.bfloat16) for _, n in ROUNDS]
        + [
            slots,
            slots,
            slots,
            pltpu.VMEM((SEQ, GROUP, 1, TILE), jnp.float32),
            pltpu.VMEM((TILES, GROUP, TILE, HD), jnp.bfloat16),
            pltpu.VMEM((TILES, GROUP, 1, TILE), jnp.float32),
            pltpu.VMEM((SEQ, 1, 128), jnp.int32),
            pltpu.SMEM((SEQ, 1, 128), jnp.int32),
            pltpu.VMEM((XN, KVN, GROUP * HD, HD), jnp.bfloat16),
            pltpu.VMEM((KVN * GROUP * HD, XN * HD), jnp.bfloat16),
            pltpu.VMEM((rows, XN * HD), jnp.float32),
            pltpu.VMEM((2, BLOCKS, BLK, HD), jnp.bfloat16),
        ]
        + [dma((rounds, SEQ))] * 2
        + [dma((SEQ,))] * 2
        + [dma((rounds, SEQ))] * 4
        + [dma((rounds, YN))] * 4
        + [dma((2, ZN))] * 2
        + [dma((ZN, XN))] * 2
        + [dma((2,))]
        + [dma((2 + rounds,))],
        compiler_params=pltpu.CompilerParams(
            collective_id=0, has_side_effects=True, vmem_limit_bytes=60 << 20
        ),
    )(
        table,
        queries.reshape(TILES, TILE, GROUP * HD),
        kv_cache.reshape(2, BLOCKS, BLK, HD),
        slot_block,
        out_weight,
    )


def solution(mesh):
    in_specs = (P("seq", "kvh"), P(None, "seq", "kvh"), P("seq", "kvh", None), P("kvh", "seq"))
    out_specs = P("seq", "kvh")
    return jax.shard_map(
        per_device, mesh=mesh, in_specs=in_specs, out_specs=out_specs, check_vma=False
    )
```

```python
import functools

import jax
import jax.numpy as jnp
from jax import lax
from jax.experimental import pallas as pl
from jax.experimental.pallas import tpu as pltpu
from jax.sharding import PartitionSpec as P

GROUP = 4
HD = 128
BLK = 1024
TILE = 128
SEL = 2
ZN = 8
XN = 4
SEQ = ZN * XN
KVN = 8
YN = 4
TILES = 8
BLOCKS = 8
SCALE = HD ** (-0.5)
LOG2E = 1.4426950408889634
MESH = pl.DeviceIdType.MESH
PARTS = ((0, 0, 128), (1, 0, 128), (2, 0, 128), (3, 0, 64), (3, 64, 64))


def to_row(column, eye):
    return jnp.sum(jnp.where(eye, column, 0.0), axis=0, keepdims=True)


def to_column(row, eye):
    return jnp.sum(jnp.where(eye, row, 0.0), axis=1, keepdims=True)


def attend(query, keys, values, visible):
    scores = lax.dot_general(
        query, keys, (((1,), (1,)), ((), ())), preferred_element_type=jnp.float32
    )
    if visible is not None:
        scores = jnp.where(visible, scores, -jnp.inf)
    top = jnp.max(scores, axis=1, keepdims=True)
    weights = jnp.exp2((scores - top) * (SCALE * LOG2E))
    total = jnp.sum(weights, axis=1, keepdims=True)
    summed = jnp.dot(
        weights.astype(jnp.bfloat16), values, preferred_element_type=jnp.float32
    )
    return (summed / total).astype(jnp.bfloat16), top * SCALE + jnp.log(total)


def fused(tab, q_ref, cache_ref, blk_ref, w_ref, out_ref, *scratch):
    parts = len(PARTS)
    in_o, att, own_att = (scratch[n * parts : (n + 1) * parts] for n in range(3))
    in_l, out_l = scratch[3 * parts : 3 * parts + GROUP], scratch[3 * parts + GROUP :][:GROUP]
    rest = scratch[3 * parts + 2 * GROUP :]
    out_q, in_q, out_o, own_o, own_l, in_blk, blk_s, wbuf, wfull, acc, kv_ref = rest[:11]
    q_send, q_recv, b_send, b_recv, o_send, o_recv, l_send, l_recv = rest[11:19]
    a_send, a_recv, s_send, s_recv, z_send, z_recv, x_send, x_recv, p_sem, local_sem = rest[19:]
    seq = lax.axis_index("seq")
    kvh = lax.axis_index("kvh")
    z, x = seq // XN, seq % XN
    y, core = kvh // 2, kvh % 2

    def ahead(shift):
        return ((z + shift // XN) % ZN) * XN + (x + shift % XN) % XN

    def behind(shift):
        return ((z + ZN - shift // XN) % ZN) * XN + (x + XN - shift % XN) % XN

    def chip(step):
        return ((y + step) % YN) * 2 + core

    sibling = y * 2 + 1 - core
    cache = pltpu.make_async_copy(cache_ref, kv_ref, local_sem.at[1 + parts])
    cache.start()

    barrier = pltpu.get_barrier_semaphore()

    def greet_seq(shift, carry):
        pl.semaphore_signal(
            barrier, inc=1, device_id={"seq": ahead(shift)}, device_id_type=MESH
        )
        return carry

    lax.fori_loop(1, SEQ, greet_seq, 0)
    for peer in [chip(1), chip(2), chip(3), sibling]:
        pl.semaphore_signal(barrier, inc=1, device_id={"kvh": peer}, device_id_type=MESH)
    partner = {"seq": kvh * XN + x, "kvh": z}

    @pl.when(kvh != z)
    def _():
        pl.semaphore_signal(barrier, inc=1, device_id=partner, device_id_type=MESH)
        pl.semaphore_wait(barrier, SEQ + YN)

    @pl.when(kvh == z)
    def _():
        pl.semaphore_wait(barrier, SEQ - 1 + YN)

    def remote(src, dst, send, recv, **device):
        return pltpu.make_async_remote_copy(
            src_ref=src,
            dst_ref=dst,
            send_sem=send,
            recv_sem=recv,
            device_id=device,
            device_id_type=MESH,
        )

    def blk_copy(shift):
        return remote(
            blk_ref.at[shift], in_blk.at[shift], b_send.at[shift], b_recv.at[shift], seq=ahead(shift)
        )

    def q_copy(head, shift):
        return remote(
            out_q.at[shift, head],
            in_q.at[shift, head],
            q_send.at[head, shift],
            q_recv.at[head, shift],
            seq=ahead(shift),
        )

    def o_copy(index, shift):
        head, first, count = PARTS[index]
        return remote(
            out_o.at[shift, head, pl.ds(first, count)],
            in_o[index].at[shift],
            o_send.at[index, shift],
            o_recv.at[index, shift],
            seq=behind(shift),
        )

    def l_copy(head, shift):
        return remote(
            out_l[head].at[shift],
            in_l[head].at[shift],
            l_send.at[head, shift],
            l_recv.at[head, shift],
            seq=behind(shift),
        )

    def lanes(group):
        return pl.ds(pl.multiple_of(group * HD, HD), HD)

    def a_copy(index, step):
        return remote(
            own_att[index],
            att[index].at[:, lanes(kvh)],
            a_send.at[index, step],
            a_recv.at[index, step],
            kvh=chip(step),
        )

    def s_copy(index, step):
        part = att[index].at[:, lanes(chip(YN - step))]
        return remote(
            own_att[index] if step == 0 else part,
            part,
            s_send.at[index, step],
            s_recv.at[index, step],
            kvh=sibling,
        )

    def z_copy(way, step):
        block = (z + ZN - step + 1) % ZN if way == 0 else (z + step - 1) % ZN
        part = wbuf.at[x, block]
        return remote(
            part,
            part,
            z_send.at[way, step],
            z_recv.at[way, step],
            seq=((z + 1) % ZN if way == 0 else (z + ZN - 1) % ZN) * XN + x,
        )

    def p_copy():
        return remote(w_ref, wbuf.at[x, kvh], p_sem.at[0], p_sem.at[1], **partner)

    def x_copy(piece, step):
        block = (z + ZN - piece) % ZN
        part = wbuf.at[x, block]
        return remote(
            part,
            part,
            x_send.at[piece, step],
            x_recv.at[piece, step],
            seq=z * XN + (x + step) % XN,
        )

    def x_start(*pieces):
        for piece in pieces:
            for step in (2, 1, 3):
                x_copy(piece, step).start()

    z_steps = (ZN // 2, ZN // 2 - 1)

    def z_start(step):
        for way in range(2):
            if step <= z_steps[way]:
                z_copy(way, step).start()

    def z_wait(step):
        for way in range(2):
            if step <= z_steps[way]:
                z_copy(way, step).wait_recv()

    def place(first, count):
        return lax.broadcasted_iota(jnp.int32, (count, TILE), 1) == (
            first + lax.broadcasted_iota(jnp.int32, (count, TILE), 0)
        )

    def own_piece(tile, carry):
        visible = lax.broadcasted_iota(jnp.int32, (TILE, BLK), 1) <= (
            tile * TILE + lax.broadcasted_iota(jnp.int32, (TILE, BLK), 0)
        )
        for head in range(GROUP):
            out, lse = attend(
                q_ref[tile, :, head * HD : (head + 1) * HD],
                kv_ref[0, BLOCKS - 1],
                kv_ref[1, BLOCKS - 1],
                visible,
            )
            own_o[tile, head] = out
            own_l[tile, head] = to_row(lse, place(0, TILE))
        return carry

    def send_blk(shift, carry):
        blk_copy(shift).start()
        return carry

    def send_queries(head):
        def pack(shift, carry):
            out_q[shift, head] = q_ref[tab[shift], :, head * HD : (head + 1) * HD]
            q_copy(head, shift).start()
            return carry

        in_q[0, head] = q_ref[tab[0], :, head * HD : (head + 1) * HD]
        lax.fori_loop(1, SEQ, pack, 0)

    def serve_head(head, between=()):
        spot = place(0, TILE)
        mine = [n for n, part in enumerate(PARTS) if part[0] == head]

        def serve(shift):
            block = blk_s[shift, 0, 0]
            out, lse = attend(in_q[shift, head], kv_ref[0, block], kv_ref[1, block], None)
            return out, to_row(lse, spot)

        def step(shift, carry):
            q_copy(head, shift).wait_recv()
            out, row = serve(shift)
            out_o[shift, head] = out
            out_l[head][shift] = row
            o_copy(mine[0], shift).start()
            l_copy(head, shift).start()
            return carry

        out, row = serve(0)
        in_l[head][0] = row
        for index in mine:
            _, first, count = PARTS[index]
            in_o[index][0] = out[first : first + count]
        cuts = [1 + (SEQ - 1) * n // (len(between) + 1) for n in range(len(between) + 2)]
        for number in range(len(cuts) - 1):
            lax.fori_loop(cuts[number], cuts[number + 1], step, 0)
            if number < len(between):
                piece, distance = between[number]
                x_copy(piece, distance).start()
        for index in mine[1:]:

            def later(shift, carry, index=index):
                o_copy(index, shift).start()
                return carry

            lax.fori_loop(1, SEQ, later, 0)

    def mix_part(index):
        head, first, count = PARTS[index]
        spot = place(first, count)

        def arrived(shift, carry):
            o_copy(index, shift).wait_recv()
            if first == 0:
                l_copy(head, shift).wait_recv()
            return carry

        lax.fori_loop(1, SEQ, arrived, 0)

        def mix(tile, carry):
            one = tab[SEQ + tile * SEL]
            two = tab[SEQ + tile * SEL + 1]
            rows = [own_l[tile, head], in_l[head][one], in_l[head][two]]
            outs = [
                own_o[tile, head, first : first + count, :],
                in_o[index][one],
                in_o[index][two],
            ]
            high = jnp.maximum(jnp.maximum(rows[0], rows[1]), rows[2])
            shares = [jnp.exp(r - high) for r in rows]
            norm = shares[0] + shares[1] + shares[2]
            blended = jnp.zeros((count, HD), jnp.float32)
            for share, out in zip(shares, outs):
                blended = blended + to_column(share / norm, spot) * out.astype(jnp.float32)
            own_att[index][pl.ds(pl.multiple_of(tile * count, count), count), :] = blended.astype(
                jnp.bfloat16
            )
            return carry

        lax.fori_loop(0, TILES, mix, 0)
        for step in range(1, YN):
            a_copy(index, step).start()
        s_copy(index, 0).start()
        keep(index).start()

    def keep(index):
        return pltpu.make_async_copy(
            own_att[index], att[index].at[:, lanes(kvh)], local_sem.at[1 + index]
        )

    def pass_on(index):
        for step in range(1, YN):
            a_copy(index, step).wait_recv()
            s_copy(index, step).start()

    def project(index):
        head, first, count = PARTS[index]
        for step in range(YN):
            s_copy(index, step).wait_recv()
        keep(index).wait()
        group = 256 // count

        def rows_of(number, carry):
            rows = pl.ds(pl.multiple_of(number * 256, 256), 256)
            term = jnp.dot(
                att[index][rows, :],
                wfull[head * KVN * HD : (head + 1) * KVN * HD, :],
                preferred_element_type=jnp.float32,
            ).reshape(group, count, XN * HD)
            target = (pl.ds(number * group, group), pl.ds(first, count))
            if head > 0:
                term = acc[target] + term
            if head == GROUP - 1:
                out_ref[target] = term.astype(jnp.bfloat16)
            else:
                acc[target] = term
            return carry

        lax.fori_loop(0, TILES // group, rows_of, 0)

    @pl.when(kvh != z)
    def _():
        p_copy().start()

    @pl.when(kvh == z)
    def _():
        wbuf[x, z] = w_ref[...]

    lax.fori_loop(1, SEQ, send_blk, 0)
    tiles = TILES // GROUP
    for index in range(GROUP):
        send_queries(index)
        if index == 0:
            cache.wait()
        if index == 1:
            x_start(0)
        if index == 2:
            x_start(1, 7)
        lax.fori_loop(index * tiles, (index + 1) * tiles, own_piece, 0)
        if index == 0:

            @pl.when(kvh != z)
            def _():
                p_copy().wait()

        else:
            z_wait(index)
        z_start(index + 1)

    def wait_blk(shift, carry):
        blk_copy(shift).wait_recv()
        return carry

    lax.fori_loop(1, SEQ, wait_blk, 0)
    in_blk[0] = blk_ref[0]
    fetch = pltpu.make_async_copy(in_blk, blk_s, local_sem.at[0])
    fetch.start()
    fetch.wait()

    serve_head(0, [(p, d) for p in (2, 6) for d in (2, 1, 3)])
    z_wait(GROUP)
    serve_head(1, [(p, d) for p in (3, 5) for d in (2, 1, 3)])
    serve_head(2, [(4, d) for d in (2, 1, 3)])
    mix_part(0)
    serve_head(3)
    mix_part(1)
    pass_on(0)

    for piece in range(ZN):
        for step in range(1, XN):
            x_copy(piece, step).wait_recv()
    for head in range(GROUP):

        def arrange(group, carry, head=head):
            row = pl.multiple_of((head * KVN + group) * HD, HD)
            for col in range(XN):
                wfull[pl.ds(row, HD), col * HD : (col + 1) * HD] = wbuf[
                    col, group, head * HD : (head + 1) * HD, :
                ]
            return carry

        lax.fori_loop(0, KVN, arrange, 0)

    mix_part(2)
    pass_on(1)
    for index in range(3, parts):
        mix_part(index)
    pass_on(2)
    project(0)
    project(1)
    for index in range(3, parts):
        pass_on(index)
    project(2)
    for index in range(3, parts):
        project(index)

    def finish_q(shift, carry):
        for head in range(GROUP):
            q_copy(head, shift).wait_send()
            l_copy(head, shift).wait_send()
        return carry

    lax.fori_loop(1, SEQ, finish_q, 0)
    for index in range(parts):

        def finish(shift, carry, index=index):
            o_copy(index, shift).wait_send()
            return carry

        lax.fori_loop(1, SEQ, finish, 0)
        for step in range(1, YN):
            a_copy(index, step).wait_send()
        for step in range(YN):
            s_copy(index, step).wait_send()

    def finish_blk(shift, carry):
        blk_copy(shift).wait_send()
        return carry

    lax.fori_loop(1, SEQ, finish_blk, 0)
    for way in range(2):
        for step in range(1, z_steps[way] + 1):
            z_copy(way, step).wait_send()
    for piece in range(ZN):
        for step in range(1, XN):
            x_copy(piece, step).wait_send()


def per_device(queries, kv_cache, selected, out_weight):
    rows = queries.shape[0]
    seq = lax.axis_index("seq")
    z, x = seq // XN, seq % XN
    own_block = seq * BLOCKS + BLOCKS - 1
    chosen = selected.reshape(TILES * SEL)
    target = jnp.where(chosen >= own_block, chosen + 1, chosen)
    holder = target // BLOCKS
    within = target % BLOCKS
    shift = ((holder // XN - z + ZN) % ZN) * XN + (holder % XN - x + XN) % XN
    routing = shift[None, :] == jnp.arange(SEQ, dtype=jnp.int32)[:, None]
    request_tile = jnp.arange(TILES * SEL, dtype=jnp.int32) // SEL
    slot_tile = jnp.sum(jnp.where(routing, request_tile[None, :], 0), axis=1)
    slot_block = jnp.sum(jnp.where(routing, within[None, :], 0), axis=1)
    table = jnp.concatenate([slot_tile, shift]).astype(jnp.int32)
    slot_block = jnp.broadcast_to(slot_block.astype(jnp.int32)[:, None, None], (SEQ, 1, 128))

    parts = len(PARTS)
    vmem = pl.BlockSpec(memory_space=pltpu.VMEM)
    dma = pltpu.SemaphoreType.DMA
    slots = pltpu.VMEM((SEQ, GROUP, TILE, HD), jnp.bfloat16)
    stats = pltpu.VMEM((SEQ, 1, TILE), jnp.float32)
    out = pl.pallas_call(
        fused,
        name="fused",
        out_shape=jax.ShapeDtypeStruct((TILES, TILE, XN * HD), jnp.bfloat16),
        in_specs=[
            pl.BlockSpec(memory_space=pltpu.SMEM),
            vmem,
            pl.BlockSpec(memory_space=pl.ANY),
            vmem,
            vmem,
        ],
        out_specs=vmem,
        scratch_shapes=[pltpu.VMEM((SEQ, n, HD), jnp.bfloat16) for _, _, n in PARTS]
        + [pltpu.VMEM((TILES * n, KVN * HD), jnp.bfloat16) for _, _, n in PARTS]
        + [pltpu.VMEM((TILES * n, HD), jnp.bfloat16) for _, _, n in PARTS]
        + [stats] * (2 * GROUP)
        + [
            slots,
            slots,
            slots,
            pltpu.VMEM((TILES, GROUP, TILE, HD), jnp.bfloat16),
            pltpu.VMEM((TILES, GROUP, 1, TILE), jnp.float32),
            pltpu.VMEM((SEQ, 1, 128), jnp.int32),
            pltpu.SMEM((SEQ, 1, 128), jnp.int32),
            pltpu.VMEM((XN, KVN, GROUP * HD, HD), jnp.bfloat16),
            pltpu.VMEM((KVN * GROUP * HD, XN * HD), jnp.bfloat16),
            pltpu.VMEM((TILES, TILE, XN * HD), jnp.float32),
            pltpu.VMEM((2, BLOCKS, BLK, HD), jnp.bfloat16),
        ]
        + [dma((GROUP, SEQ))] * 2
        + [dma((SEQ,))] * 2
        + [dma((parts, SEQ))] * 2
        + [dma((GROUP, SEQ))] * 2
        + [dma((parts, YN))] * 4
        + [dma((2, ZN))] * 2
        + [dma((ZN, XN))] * 2
        + [dma((2,))]
        + [dma((2 + parts,))],
        compiler_params=pltpu.CompilerParams(
            collective_id=0, has_side_effects=True, vmem_limit_bytes=60 << 20
        ),
    )(
        table,
        queries.reshape(TILES, TILE, GROUP * HD),
        kv_cache.reshape(2, BLOCKS, BLK, HD),
        slot_block,
        out_weight,
    )
    return out.reshape(rows, XN * HD)


def solution(mesh):
    in_specs = (P("seq", "kvh"), P(None, "seq", "kvh"), P("seq", "kvh", None), P("kvh", "seq"))
    out_specs = P("seq", "kvh")
    return jax.shard_map(
        per_device, mesh=mesh, in_specs=in_specs, out_specs=out_specs, check_vma=False
    )
```

```python
import functools

import jax
import jax.numpy as jnp
from jax import lax
from jax.experimental import pallas as pl
from jax.experimental.pallas import tpu as pltpu
from jax.sharding import PartitionSpec as P

GROUP = 4
HD = 128
BLK = 1024
TILE = 128
SEL = 2
ZN = 8
XN = 4
SEQ = ZN * XN
KVN = 8
YN = 4
TILES = 8
BLOCKS = 8
SCALE = HD ** (-0.5)
LOG2E = 1.4426950408889634
MESH = pl.DeviceIdType.MESH
PARTS = ((0, 0, 128), (1, 0, 128), (2, 0, 128), (3, 0, 64), (3, 64, 64))


def to_row(column, eye):
    return jnp.sum(jnp.where(eye, column, 0.0), axis=0, keepdims=True)


def to_column(row, eye):
    return jnp.sum(jnp.where(eye, row, 0.0), axis=1, keepdims=True)


def attend(query, keys, values, visible):
    scores = lax.dot_general(
        query, keys, (((1,), (1,)), ((), ())), preferred_element_type=jnp.float32
    )
    if visible is not None:
        scores = jnp.where(visible, scores, -jnp.inf)
    top = jnp.max(scores, axis=1, keepdims=True)
    weights = jnp.exp2((scores - top) * (SCALE * LOG2E))
    total = jnp.sum(weights, axis=1, keepdims=True)
    summed = jnp.dot(
        weights.astype(jnp.bfloat16), values, preferred_element_type=jnp.float32
    )
    return (summed / total).astype(jnp.bfloat16), top * SCALE + jnp.log(total)


def fused(tab, q_ref, cache_ref, blk_ref, w_ref, out_ref, *scratch):
    parts = len(PARTS)
    in_o, att, own_att = (scratch[n * parts : (n + 1) * parts] for n in range(3))
    in_l, out_l = scratch[3 * parts : 3 * parts + GROUP], scratch[3 * parts + GROUP :][:GROUP]
    rest = scratch[3 * parts + 2 * GROUP :]
    out_q, in_q, out_o, own_o, own_l, in_blk, blk_s, wbuf, wfull, acc, kv_ref = rest[:11]
    q_send, q_recv, b_send, b_recv, o_send, o_recv, l_send, l_recv = rest[11:19]
    a_send, a_recv, s_send, s_recv, z_send, z_recv, x_send, x_recv, p_sem, local_sem = rest[19:]
    seq = lax.axis_index("seq")
    kvh = lax.axis_index("kvh")
    z, x = seq // XN, seq % XN
    y, core = kvh // 2, kvh % 2

    def ahead(shift):
        return ((z + shift // XN) % ZN) * XN + (x + shift % XN) % XN

    def behind(shift):
        return ((z + ZN - shift // XN) % ZN) * XN + (x + XN - shift % XN) % XN

    def chip(step):
        return ((y + step) % YN) * 2 + core

    sibling = y * 2 + 1 - core
    cache = pltpu.make_async_copy(cache_ref, kv_ref, local_sem.at[1 + parts])
    cache.start()

    barrier = pltpu.get_barrier_semaphore()

    def greet_seq(shift, carry):
        pl.semaphore_signal(
            barrier, inc=1, device_id={"seq": ahead(shift)}, device_id_type=MESH
        )
        return carry

    lax.fori_loop(1, SEQ, greet_seq, 0)
    for peer in [chip(1), chip(2), chip(3), sibling]:
        pl.semaphore_signal(barrier, inc=1, device_id={"kvh": peer}, device_id_type=MESH)
    partner = {"seq": kvh * XN + x, "kvh": z}

    @pl.when(kvh != z)
    def _():
        pl.semaphore_signal(barrier, inc=1, device_id=partner, device_id_type=MESH)
        pl.semaphore_wait(barrier, SEQ + YN)

    @pl.when(kvh == z)
    def _():
        pl.semaphore_wait(barrier, SEQ - 1 + YN)

    def remote(src, dst, send, recv, **device):
        return pltpu.make_async_remote_copy(
            src_ref=src,
            dst_ref=dst,
            send_sem=send,
            recv_sem=recv,
            device_id=device,
            device_id_type=MESH,
        )

    def blk_copy(shift):
        return remote(
            blk_ref.at[shift], in_blk.at[shift], b_send.at[shift], b_recv.at[shift], seq=ahead(shift)
        )

    def q_copy(head, shift):
        return remote(
            out_q.at[shift, head],
            in_q.at[shift, head],
            q_send.at[head, shift],
            q_recv.at[head, shift],
            seq=ahead(shift),
        )

    def o_copy(index, shift):
        head, first, count = PARTS[index]
        return remote(
            out_o.at[shift, head, pl.ds(first, count)],
            in_o[index].at[shift],
            o_send.at[index, shift],
            o_recv.at[index, shift],
            seq=behind(shift),
        )

    def l_copy(head, shift):
        return remote(
            out_l[head].at[shift],
            in_l[head].at[shift],
            l_send.at[head, shift],
            l_recv.at[head, shift],
            seq=behind(shift),
        )

    def lanes(group):
        return pl.ds(pl.multiple_of(group * HD, HD), HD)

    def a_copy(index, step):
        return remote(
            own_att[index],
            att[index].at[:, lanes(kvh)],
            a_send.at[index, step],
            a_recv.at[index, step],
            kvh=chip(step),
        )

    def s_copy(index, step):
        part = att[index].at[:, lanes(chip(YN - step))]
        return remote(
            own_att[index] if step == 0 else part,
            part,
            s_send.at[index, step],
            s_recv.at[index, step],
            kvh=sibling,
        )

    def z_copy(way, step):
        block = (z + ZN - step + 1) % ZN if way == 0 else (z + step - 1) % ZN
        part = wbuf.at[x, block]
        return remote(
            part,
            part,
            z_send.at[way, step],
            z_recv.at[way, step],
            seq=((z + 1) % ZN if way == 0 else (z + ZN - 1) % ZN) * XN + x,
        )

    def p_copy():
        return remote(w_ref, wbuf.at[x, kvh], p_sem.at[0], p_sem.at[1], **partner)

    def x_copy(piece, step):
        block = (z + ZN - piece) % ZN
        part = wbuf.at[x, block]
        return remote(
            part,
            part,
            x_send.at[piece, step],
            x_recv.at[piece, step],
            seq=z * XN + (x + step) % XN,
        )

    def x_start(*pieces):
        for piece in pieces:
            for step in (2, 1, 3):
                x_copy(piece, step).start()

    z_steps = (ZN // 2, ZN // 2 - 1)

    def z_start(step):
        for way in range(2):
            if step <= z_steps[way]:
                z_copy(way, step).start()

    def z_wait(step):
        for way in range(2):
            if step <= z_steps[way]:
                z_copy(way, step).wait_recv()

    def place(first, count):
        return lax.broadcasted_iota(jnp.int32, (count, TILE), 1) == (
            first + lax.broadcasted_iota(jnp.int32, (count, TILE), 0)
        )

    def own_piece(tile, carry):
        visible = lax.broadcasted_iota(jnp.int32, (TILE, BLK), 1) <= (
            tile * TILE + lax.broadcasted_iota(jnp.int32, (TILE, BLK), 0)
        )
        for head in range(GROUP):
            out, lse = attend(
                q_ref[tile, :, head * HD : (head + 1) * HD],
                kv_ref[0, BLOCKS - 1],
                kv_ref[1, BLOCKS - 1],
                visible,
            )
            own_o[tile, head] = out
            own_l[tile, head] = to_row(lse, place(0, TILE))
        return carry

    def send_blk(shift, carry):
        blk_copy(shift).start()
        return carry

    def send_queries(head):
        def pack(shift, carry):
            out_q[shift, head] = q_ref[tab[shift], :, head * HD : (head + 1) * HD]
            q_copy(head, shift).start()
            return carry

        in_q[0, head] = q_ref[tab[0], :, head * HD : (head + 1) * HD]
        lax.fori_loop(1, SEQ, pack, 0)

    def serve_head(head, between=()):
        spot = place(0, TILE)
        mine = [n for n, part in enumerate(PARTS) if part[0] == head]

        def serve(shift):
            block = blk_s[shift, 0, 0]
            out, lse = attend(in_q[shift, head], kv_ref[0, block], kv_ref[1, block], None)
            return out, to_row(lse, spot)

        def step(shift, carry):
            q_copy(head, shift).wait_recv()
            out, row = serve(shift)
            out_o[shift, head] = out
            out_l[head][shift] = row
            o_copy(mine[0], shift).start()
            l_copy(head, shift).start()
            return carry

        out, row = serve(0)
        in_l[head][0] = row
        for index in mine:
            _, first, count = PARTS[index]
            in_o[index][0] = out[first : first + count]
        cuts = [1 + (SEQ - 1) * n // (len(between) + 1) for n in range(len(between) + 2)]
        for number in range(len(cuts) - 1):
            lax.fori_loop(cuts[number], cuts[number + 1], step, 0)
            if number < len(between):
                piece, distance = between[number]
                x_copy(piece, distance).start()
        for index in mine[1:]:

            def later(shift, carry, index=index):
                o_copy(index, shift).start()
                return carry

            lax.fori_loop(1, SEQ, later, 0)

    def mix_part(index):
        head, first, count = PARTS[index]
        spot = place(first, count)

        def arrived(shift, carry):
            o_copy(index, shift).wait_recv()
            if first == 0:
                l_copy(head, shift).wait_recv()
            return carry

        lax.fori_loop(1, SEQ, arrived, 0)

        def mix(tile, carry):
            one = tab[SEQ + tile * SEL]
            two = tab[SEQ + tile * SEL + 1]
            rows = [own_l[tile, head], in_l[head][one], in_l[head][two]]
            outs = [
                own_o[tile, head, first : first + count, :],
                in_o[index][one],
                in_o[index][two],
            ]
            high = jnp.maximum(jnp.maximum(rows[0], rows[1]), rows[2])
            shares = [jnp.exp(r - high) for r in rows]
            norm = shares[0] + shares[1] + shares[2]
            blended = jnp.zeros((count, HD), jnp.float32)
            for share, out in zip(shares, outs):
                blended = blended + to_column(share / norm, spot) * out.astype(jnp.float32)
            own_att[index][pl.ds(pl.multiple_of(tile * count, count), count), :] = blended.astype(
                jnp.bfloat16
            )
            return carry

        lax.fori_loop(0, TILES, mix, 0)
        for step in (2, 1, 3):
            a_copy(index, step).start()
        s_copy(index, 0).start()
        keep(index).start()

    def keep(index):
        return pltpu.make_async_copy(
            own_att[index], att[index].at[:, lanes(kvh)], local_sem.at[1 + index]
        )

    def pass_on(index):
        for step in (1, 3, 2):
            a_copy(index, step).wait_recv()
            s_copy(index, step).start()

    def project(index):
        head, first, count = PARTS[index]
        for step in range(YN):
            s_copy(index, step).wait_recv()
        keep(index).wait()
        group = 256 // count

        def rows_of(number, carry):
            rows = pl.ds(pl.multiple_of(number * 256, 256), 256)
            term = jnp.dot(
                att[index][rows, :],
                wfull[head * KVN * HD : (head + 1) * KVN * HD, :],
                preferred_element_type=jnp.float32,
            ).reshape(group, count, XN * HD)
            target = (pl.ds(number * group, group), pl.ds(first, count))
            if head > 0:
                term = acc[target] + term
            if head == GROUP - 1:
                out_ref[target] = term.astype(jnp.bfloat16)
            else:
                acc[target] = term
            return carry

        lax.fori_loop(0, TILES // group, rows_of, 0)

    @pl.when(kvh != z)
    def _():
        p_copy().start()

    @pl.when(kvh == z)
    def _():
        wbuf[x, z] = w_ref[...]

    lax.fori_loop(1, SEQ, send_blk, 0)
    tiles = TILES // GROUP
    for index in range(GROUP):
        send_queries(index)
        if index == 0:
            cache.wait()
        if index == 1:
            x_start(0)
        if index == 2:
            x_start(1, 7)
        lax.fori_loop(index * tiles, (index + 1) * tiles, own_piece, 0)
        if index == 0:

            @pl.when(kvh != z)
            def _():
                p_copy().wait()

        else:
            z_wait(index)
        z_start(index + 1)

    def wait_blk(shift, carry):
        blk_copy(shift).wait_recv()
        return carry

    lax.fori_loop(1, SEQ, wait_blk, 0)
    in_blk[0] = blk_ref[0]
    fetch = pltpu.make_async_copy(in_blk, blk_s, local_sem.at[0])
    fetch.start()
    fetch.wait()

    serve_head(0, [(p, d) for p in (2, 6) for d in (2, 1, 3)])
    z_wait(GROUP)
    serve_head(1, [(p, d) for p in (3, 5) for d in (2, 1, 3)])
    serve_head(2, [(4, d) for d in (2, 1, 3)])
    mix_part(0)
    serve_head(3)
    mix_part(1)
    pass_on(0)

    for piece in range(ZN):
        for step in range(1, XN):
            x_copy(piece, step).wait_recv()
    for head in range(GROUP):

        def arrange(group, carry, head=head):
            row = pl.multiple_of((head * KVN + group) * HD, HD)
            for col in range(XN):
                wfull[pl.ds(row, HD), col * HD : (col + 1) * HD] = wbuf[
                    col, group, head * HD : (head + 1) * HD, :
                ]
            return carry

        lax.fori_loop(0, KVN, arrange, 0)

    mix_part(2)
    pass_on(1)
    for index in range(3, parts):
        mix_part(index)
    pass_on(2)
    pass_on(3)
    project(0)
    project(1)
    for index in range(4, parts):
        pass_on(index)
    project(2)
    for index in range(3, parts):
        project(index)

    def finish_q(shift, carry):
        for head in range(GROUP):
            q_copy(head, shift).wait_send()
            l_copy(head, shift).wait_send()
        return carry

    lax.fori_loop(1, SEQ, finish_q, 0)
    for index in range(parts):

        def finish(shift, carry, index=index):
            o_copy(index, shift).wait_send()
            return carry

        lax.fori_loop(1, SEQ, finish, 0)
        for step in range(1, YN):
            a_copy(index, step).wait_send()
        for step in range(YN):
            s_copy(index, step).wait_send()

    def finish_blk(shift, carry):
        blk_copy(shift).wait_send()
        return carry

    lax.fori_loop(1, SEQ, finish_blk, 0)
    for way in range(2):
        for step in range(1, z_steps[way] + 1):
            z_copy(way, step).wait_send()
    for piece in range(ZN):
        for step in range(1, XN):
            x_copy(piece, step).wait_send()


def per_device(queries, kv_cache, selected, out_weight):
    rows = queries.shape[0]
    seq = lax.axis_index("seq")
    z, x = seq // XN, seq % XN
    own_block = seq * BLOCKS + BLOCKS - 1
    chosen = selected.reshape(TILES * SEL)
    target = jnp.where(chosen >= own_block, chosen + 1, chosen)
    holder = target // BLOCKS
    within = target % BLOCKS
    shift = ((holder // XN - z + ZN) % ZN) * XN + (holder % XN - x + XN) % XN
    routing = shift[None, :] == jnp.arange(SEQ, dtype=jnp.int32)[:, None]
    request_tile = jnp.arange(TILES * SEL, dtype=jnp.int32) // SEL
    slot_tile = jnp.sum(jnp.where(routing, request_tile[None, :], 0), axis=1)
    slot_block = jnp.sum(jnp.where(routing, within[None, :], 0), axis=1)
    table = jnp.concatenate([slot_tile, shift]).astype(jnp.int32)
    slot_block = jnp.broadcast_to(slot_block.astype(jnp.int32)[:, None, None], (SEQ, 1, 128))

    parts = len(PARTS)
    vmem = pl.BlockSpec(memory_space=pltpu.VMEM)
    dma = pltpu.SemaphoreType.DMA
    slots = pltpu.VMEM((SEQ, GROUP, TILE, HD), jnp.bfloat16)
    stats = pltpu.VMEM((SEQ, 1, TILE), jnp.float32)
    out = pl.pallas_call(
        fused,
        name="fused",
        out_shape=jax.ShapeDtypeStruct((TILES, TILE, XN * HD), jnp.bfloat16),
        in_specs=[
            pl.BlockSpec(memory_space=pltpu.SMEM),
            vmem,
            pl.BlockSpec(memory_space=pl.ANY),
            vmem,
            vmem,
        ],
        out_specs=vmem,
        scratch_shapes=[pltpu.VMEM((SEQ, n, HD), jnp.bfloat16) for _, _, n in PARTS]
        + [pltpu.VMEM((TILES * n, KVN * HD), jnp.bfloat16) for _, _, n in PARTS]
        + [pltpu.VMEM((TILES * n, HD), jnp.bfloat16) for _, _, n in PARTS]
        + [stats] * (2 * GROUP)
        + [
            slots,
            slots,
            slots,
            pltpu.VMEM((TILES, GROUP, TILE, HD), jnp.bfloat16),
            pltpu.VMEM((TILES, GROUP, 1, TILE), jnp.float32),
            pltpu.VMEM((SEQ, 1, 128), jnp.int32),
            pltpu.SMEM((SEQ, 1, 128), jnp.int32),
            pltpu.VMEM((XN, KVN, GROUP * HD, HD), jnp.bfloat16),
            pltpu.VMEM((KVN * GROUP * HD, XN * HD), jnp.bfloat16),
            pltpu.VMEM((TILES, TILE, XN * HD), jnp.float32),
            pltpu.VMEM((2, BLOCKS, BLK, HD), jnp.bfloat16),
        ]
        + [dma((GROUP, SEQ))] * 2
        + [dma((SEQ,))] * 2
        + [dma((parts, SEQ))] * 2
        + [dma((GROUP, SEQ))] * 2
        + [dma((parts, YN))] * 4
        + [dma((2, ZN))] * 2
        + [dma((ZN, XN))] * 2
        + [dma((2,))]
        + [dma((2 + parts,))],
        compiler_params=pltpu.CompilerParams(
            collective_id=0, has_side_effects=True, vmem_limit_bytes=60 << 20
        ),
    )(
        table,
        queries.reshape(TILES, TILE, GROUP * HD),
        kv_cache.reshape(2, BLOCKS, BLK, HD),
        slot_block,
        out_weight,
    )
    return out.reshape(rows, XN * HD)


def solution(mesh):
    in_specs = (P("seq", "kvh"), P(None, "seq", "kvh"), P("seq", "kvh", None), P("kvh", "seq"))
    out_specs = P("seq", "kvh")
    return jax.shard_map(
        per_device, mesh=mesh, in_specs=in_specs, out_specs=out_specs, check_vma=False
    )
```
